256 devices in a mesh: rep: 8 (over y_lo, x), seq: 32 (over y_hi, z, core).
Axes of the slice: x: 4, y: 4 (y_hi: 2, y_lo: 2; y = y_hi * 2 + y_lo), z: 8, core: 2. Of those that a mesh axis runs over, the one named last changes fastest.
Arguments:
- queries: bfloat16 [8, 4096, 3072], P('rep', 'seq'), may hold values from -6 to 6
- keys: bfloat16 [8, 4096, 128], P('rep', 'seq'), may hold values from -6 to 6
- values: bfloat16 [8, 4096, 128], P('rep', 'seq'), may hold values from -6 to 6
- outputs: bfloat16 [8, 4096, 3072], P('rep', 'seq'), may hold values from -6 to 6
- out_grad: bfloat16 [8, 4096, 3072], P('rep', 'seq'), may hold values from -24 to 24
- log_norm: float32 [8, 24, 4096], P('rep', None, 'seq'), may hold values from 7 to 8.5
- inputs: bfloat16 [8, 4096, 6144], P('rep', 'seq'), may hold values from -0.29882812 to 0.29882812
- mlp_weight: bfloat16 [8, 12288, 6144], P('rep', 'seq'), may hold values from -0.0546875 to 0.0546875
- initial_right_factor: bfloat16 [32, 4, 6144], P('seq'), may hold values from -6 to 6
Outputs:
- query_grad: float32 [8, 4096, 3072], P('rep', 'seq')
- kv_grad: float32 [8, 4096, 256], P('rep', 'seq')
- proj_grad: float32 [8, 6144, 256], P('rep', 'seq')
- left_factor: float32 [8, 2, 4, 12288], P('rep', None, None, 'seq')
- right_factor: float32 [8, 32, 2, 4, 6144], P('rep', 'seq')
The draws below stay inside these ranges and needn't reach their ends.
All inputs are finite; a program needn't handle non-finite values.
Results may differ from the reference program's by a relative error of at most 0.004.
Values may be sent and summed in bfloat16 or wider, within the bound.
A program may use at most 128 MiB of HBM per device.

```python
import jax
import jax.numpy as jnp
from jax import lax

D = 6144
HEADS = 24
HD = 128
FF = 12288
WINDOW = 2048
RANK = 4
TOK_DEV = 128
SEQUENCE_LENGTH = 4096
BLOCK_ROWS = 384
N_REP = 8
N_SEQ = 32


def spiked(values, stream_key, source, target, blocks, factor):
    def block_of(dim):
        return (jnp.arange(values.shape[dim]) // (values.shape[dim] // blocks)).reshape((-1,) + (1,) * (values.ndim - 1 - dim))

    one_side = jax.random.permutation(stream_key, blocks)[block_of(target)]
    far = (block_of(target) + blocks // 2) % blocks
    return jnp.where((block_of(source) == one_side) | (block_of(source) == far), factor * values, values)


def levels(own_key, extent, shards, smallest, high):
    factor_of = 1.0
    for position, parts in shards:
        draws = jax.random.uniform(jax.random.fold_in(jax.random.fold_in(own_key, 6), position), (parts,), jnp.float32, smallest / len(shards), high / len(shards))
        factor_of = factor_of * jnp.repeat(jnp.exp(draws), extent[position] // parts).reshape((-1,) + (1,) * (len(extent) - 1 - position))
    return factor_of


def normal_values(key, dims, deviation, bound, cuts=(), held_as=jnp.bfloat16):
    gain = levels(key, dims, cuts, -0.22, 0.18) if cuts else 1.0
    drawn = jax.random.normal(key, dims, jnp.float32) * deviation * gain
    return jnp.minimum(jnp.maximum(drawn, -bound), bound).astype(held_as)


def heavy_noise(rng, shape, spread, limit, pieces, heavy, held_as=jnp.bfloat16):
    entries = spread * jax.random.normal(rng, shape, jnp.float32)
    if pieces:
        entries = entries * levels(rng, shape, pieces, -0.22, 0.18)
    return jnp.clip(spiked(entries, jax.random.fold_in(rng, 3), *heavy), -limit, limit).astype(held_as)


def setup_inputs(seed: int = 0) -> dict:
    seeds = jax.random.split(jax.random.key(seed), 10)
    queries = normal_values(seeds[0], (N_REP, SEQUENCE_LENGTH, HEADS * HD), 1.0, 6.0, ((0, 8), (1, 32)))
    keys = normal_values(seeds[1], (N_REP, SEQUENCE_LENGTH, HD), 1.0, 6.0, ((0, 8), (1, 32)))
    values = normal_values(seeds[2], (N_REP, SEQUENCE_LENGTH, HD), 1.0, 6.0, ((0, 8), (1, 32)))
    outputs = normal_values(seeds[3], (N_REP, SEQUENCE_LENGTH, HEADS * HD), 1.0, 6.0, ((0, 8), (1, 32)))
    out_grad = normal_values(seeds[4], (N_REP, SEQUENCE_LENGTH, HEADS * HD), 4.0, 24.0, ((0, 8), (1, 32)))
    log_norm = jnp.clip(7.0 + 1.5 * jax.random.uniform(seeds[5], (N_REP, HEADS, SEQUENCE_LENGTH), jnp.float32) ** levels(seeds[5], (N_REP, HEADS, SEQUENCE_LENGTH), ((0, 8), (2, 32)), -0.2, 0.2), 7.0, 8.5)
    inputs = heavy_noise(seeds[6], (N_REP, SEQUENCE_LENGTH, D), 0.05, 0.29882812, ((0, 8), (1, 32)), (1, 2, 32, 2.75))
    mlp_weight = normal_values(seeds[7], (N_REP, FF, D), FF ** -0.5, 0.0546875, ((0, 8), (1, 32)))
    initial_right_factor = normal_values(seeds[8], (N_SEQ, RANK, D), 1.0, 6.0, ((0, 32),))
    return {"queries": queries, "keys": keys, "values": values, "outputs": outputs, "out_grad": out_grad, "log_norm": log_norm, "inputs": inputs, "mlp_weight": mlp_weight, "initial_right_factor": initial_right_factor}


epsilon = 1e-06

def window_mask(first_query, row_count, span):
    query_pos = first_query + jnp.arange(row_count, dtype=jnp.int32)
    key_pos = first_query - span + jnp.arange(span + row_count, dtype=jnp.int32)
    lower_ok = key_pos[None, :] > query_pos[:, None] - span
    upper_ok = key_pos[None, :] <= query_pos[:, None]
    return (key_pos[None, :] >= 0) & lower_ok & upper_ok

def attend(query_blk, gradient_block, out_blk, norm_block, window_kv, visible, scale):
    row_count, model_cols = query_blk.shape
    head_count = norm_block.shape[0]
    width = model_cols // head_count
    group = 8 if head_count % 8 == 0 else head_count
    groups = head_count // group

    def head_rows(source):
        return source.reshape(row_count, head_count, width).transpose(1, 0, 2).reshape(groups, group * row_count, width)
    query_rows = head_rows(query_blk)
    grad_rows = head_rows(gradient_block)
    delta_all = lax.optimization_barrier(jnp.sum(gradient_block.astype(jnp.float32).reshape(row_count, head_count, width) * out_blk.astype(jnp.float32).reshape(row_count, head_count, width), axis=-1))
    delta_rows = delta_all.T.reshape(groups, group * row_count)
    norm_rows = norm_block.reshape(groups, group, row_count)
    key_mat = window_kv[:, :width]
    value_mat = window_kv[:, width:]

    def per_group(accum, items):
        query_grp, grad_grp, norm_grp, delta_grp = items
        scores = jnp.dot(query_grp, key_mat.T, preferred_element_type=jnp.float32) * scale
        scores = scores.reshape(group, row_count, -1)
        probs = jnp.where(visible[None], jnp.exp(scores - norm_grp[:, :, None]), 0.0)
        probs = probs.reshape(group * row_count, -1)
        probs_b = probs.astype(jnp.bfloat16)
        value_grad = jnp.dot(probs_b.T, grad_grp, preferred_element_type=jnp.float32)
        prob_grad = jnp.dot(grad_grp, value_mat.T, preferred_element_type=jnp.float32)
        score_grad = (scale * probs * (prob_grad - delta_grp[:, None])).astype(jnp.bfloat16)
        query_grad = jnp.dot(score_grad, key_mat, preferred_element_type=jnp.float32)
        key_grad = jnp.dot(score_grad.T, query_grp, preferred_element_type=jnp.float32)
        return (accum + jnp.concatenate([key_grad, value_grad], axis=-1), query_grad)
    start_accum = jnp.zeros((window_kv.shape[0], 2 * width), jnp.float32)
    accum, query_grads = lax.scan(per_group, start_accum, (query_rows, grad_rows, norm_rows, delta_rows))
    query_grad = query_grads.reshape(head_count, row_count, width).transpose(1, 0, 2).reshape(row_count, model_cols)
    return (query_grad, accum)

def orthonormal(diffs):
    columns = []
    for index in range(diffs.shape[-2]):
        source = diffs[..., index, :]
        vector = source
        for previous in columns:
            vector = vector - lax.optimization_barrier(jnp.mean(source * previous, axis=-1, keepdims=True)) * previous
        columns.append(vector * lax.rsqrt(lax.optimization_barrier(jnp.mean(vector * vector, axis=-1, keepdims=True)) + epsilon))
    return jnp.stack(columns, axis=-2)

def reference(queries, keys, values, outputs, out_grad, log_norm, inputs, mlp_weight, initial_right_factor):
    scale = HD ** (-0.5)

    def single_replica(items):
        query_matrix, key_all, value_all, out_all, grad_all, norm_all, input_all = items
        joined = jnp.concatenate([key_all, value_all], axis=-1)
        padded = jnp.concatenate([jnp.zeros((WINDOW, 2 * HD), joined.dtype), joined], axis=0)

        def one_block(accum, block_index):
            first = block_index * TOK_DEV
            window_kv = lax.dynamic_slice_in_dim(padded, first, WINDOW + TOK_DEV, 0)
            query_blk = lax.dynamic_slice_in_dim(query_matrix, first, TOK_DEV, 0)
            gradient_block = lax.dynamic_slice_in_dim(grad_all, first, TOK_DEV, 0)
            out_blk = lax.dynamic_slice_in_dim(out_all, first, TOK_DEV, 0)
            norm_block = lax.dynamic_slice_in_dim(norm_all, first, TOK_DEV, 1)
            visible = window_mask(first, TOK_DEV, WINDOW)
            query_grad, window_grads = attend(query_blk, gradient_block, out_blk, norm_block, window_kv, visible, scale)
            current = lax.dynamic_slice_in_dim(accum, first, WINDOW + TOK_DEV, 0)
            accum = lax.dynamic_update_slice_in_dim(accum, current + window_grads, first, 0)
            return (accum, query_grad)
        start_accum = jnp.zeros((WINDOW + SEQUENCE_LENGTH, 2 * HD), jnp.float32)
        accum, query_grads = lax.scan(one_block, start_accum, jnp.arange(N_SEQ, dtype=jnp.int32))
        kv_grad = accum[WINDOW:]
        proj_grad = jnp.dot(input_all.T, kv_grad.astype(jnp.bfloat16), preferred_element_type=jnp.float32)
        return (query_grads.reshape(SEQUENCE_LENGTH, HEADS * HD), kv_grad, proj_grad)
    query_grad, kv_grad, proj_grad = lax.map(single_replica, (queries, keys, values, outputs, out_grad, log_norm, inputs))
    blocks = mlp_weight.reshape(N_REP, N_SEQ, BLOCK_ROWS, D)

    def project(weight_row_blocks):
        return jnp.einsum('chi,cei->che', initial_right_factor.astype(jnp.float32), weight_row_blocks.astype(jnp.float32))
    acts = lax.map(project, blocks)
    lower_diff = acts - jnp.roll(acts, 1, axis=0)
    higher_diff = acts - jnp.roll(acts, -1, axis=0)
    diffs = jnp.stack([lower_diff, higher_diff], axis=2)
    basis = orthonormal(diffs)
    left_factor = basis.transpose(0, 2, 3, 1, 4).reshape(N_REP, 2, RANK, FF)
    basis_b = basis.astype(jnp.bfloat16)

    def contract(items):
        basis_rep, weight_row_blocks = items
        return jnp.einsum('bekr,brd->bekd', basis_rep.astype(jnp.float32), weight_row_blocks.astype(jnp.float32))
    contrib = lax.map(contract, (basis_b, blocks))
    lower_edge = contrib[:, :, 0] + jnp.roll(contrib[:, :, 1], 1, axis=0)
    higher_edge = contrib[:, :, 1] + jnp.roll(contrib[:, :, 0], -1, axis=0)
    right_factor = jnp.stack([lower_edge, higher_edge], axis=2)
    return (query_grad, kv_grad, proj_grad, left_factor, right_factor)
```

```python
import functools

import jax
import jax.numpy as jnp
from jax import lax
from jax.experimental import pallas as pl
from jax.experimental.pallas import tpu as pltpu
from jax.sharding import PartitionSpec as P

MESH = pl.DeviceIdType.MESH
F32 = jnp.float32
BF16 = jnp.bfloat16
EPS = 1e-06
NT = (((1,), (1,)), ((), ()))

HD = 128
HEADS = 24
TOK = 128
SPAN = 8
ROWS = 384
HALF = 192
WINDOW = 2048


def kernel(
    q_hbm, k_hbm, v_hbm, o_hbm, g_hbm, lse_hbm, x_hbm, w_hbm, f_hbm,
    dq_out, kv_out, proj_out, left_out, right_out,
    q_in, g_in, o_in, lse_in, w_in, f_in,
    q_rows, g_rows, q_cols, g_cols, lse_b, delta_b, dq_acc, bias,
    kv_buf, part, pin, gsend, grecv, own, x_all, kg, psend, precv,
    acts, acts_in, contrib, contrib_in,
    load_sem, kv_s, kv_r, fw_s, fw_r, pt_s, pt_r, gr_s, gr_r,
    x_s, x_r, kg_s, kg_r, pr_s, pr_r, a_s, a_r, c_s, c_r, dq_s,
):
    rep = lax.axis_index("rep")
    seq = lax.axis_index("seq")
    core = seq % 2
    chip = seq // 2
    half = chip // 8
    zpos = chip % 8
    mate = seq + 1 - 2 * core
    lower = (rep + 7) % 8
    higher = (rep + 1) % 8
    me = 2 * half + core

    def dev(s):
        return (rep, s)

    def remote(src, dst, ss, rs, target):
        return pltpu.make_async_remote_copy(
            src_ref=src, dst_ref=dst, send_sem=ss, recv_sem=rs,
            device_id=target, device_id_type=MESH,
        )

    barrier = pltpu.get_barrier_semaphore()

    def greet(i, _):
        pl.semaphore_signal(barrier, inc=1, device_id=dev((seq + i) % 32), device_id_type=MESH)
        return 0

    own_rows = pl.ds(pl.multiple_of(core * TOK, TOK), TOK)
    loads = [
        pltpu.make_async_copy(k_hbm.at[0], kv_buf.at[0, own_rows, pl.ds(0, HD)], load_sem.at[0]),
        pltpu.make_async_copy(v_hbm.at[0], kv_buf.at[0, own_rows, pl.ds(HD, HD)], load_sem.at[1]),
        pltpu.make_async_copy(q_hbm.at[0], q_in, load_sem.at[2]),
        pltpu.make_async_copy(g_hbm.at[0], g_in, load_sem.at[3]),
        pltpu.make_async_copy(o_hbm.at[0], o_in, load_sem.at[4]),
        pltpu.make_async_copy(lse_hbm.at[0], lse_in, load_sem.at[5]),
        pltpu.make_async_copy(f_hbm.at[0], f_in, load_sem.at[6]),
        pltpu.make_async_copy(w_hbm.at[0], w_in, load_sem.at[7]),
    ]
    for load in loads:
        load.start()
    lax.fori_loop(1, 32, greet, 0)
    for other in (lower, higher):
        pl.semaphore_signal(barrier, inc=1, device_id=(other, seq), device_id_type=MESH)
    pl.semaphore_wait(barrier, 33)

    loads[0].wait()
    loads[1].wait()

    def kv_copy(j):
        return remote(
            kv_buf.at[0, own_rows, :], kv_buf.at[j, own_rows, :],
            kv_s.at[j], kv_r.at[j], dev(seq + 2 * j),
        )

    def forward(j):
        return remote(
            kv_buf.at[j, own_rows, :], kv_buf.at[j, own_rows, :],
            fw_s.at[j], fw_r.at[j], dev(mate),
        )

    forward(0).start()

    def kv_send(j, _):
        @pl.when(chip + j <= 15)
        def _():
            kv_copy(j).start()

        return 0

    lax.fori_loop(1, SPAN + 1, kv_send, 0)

    def x_slot(m, i):
        return x_all.at[
            pl.ds(pl.multiple_of(m * TOK, TOK), TOK), pl.ds(pl.multiple_of(i * ROWS, ROWS), ROWS)
        ]

    def x_copy(n, local):
        m, i = n // 4, n % 4
        block = 8 * (m // 2) + 2 * i + m % 2
        src = x_hbm.at[0, :, pl.ds(pl.multiple_of(block * ROWS, ROWS), ROWS)]
        if local:
            return pltpu.make_async_copy(src, x_slot(me, i), x_r.at[n])
        return remote(
            src, x_slot(me, i), x_s.at[n], x_r.at[4 * me + i],
            dev(16 * (m // 2) + 2 * zpos + m % 2),
        )

    def x_send(n, _):
        @pl.when(n // 4 == me)
        def _():
            x_copy(n, True).start()

        @pl.when(n // 4 != me)
        def _():
            x_copy(n, False).start()

        return 0

    lax.fori_loop(0, 16, x_send, 0)

    loads[2].wait()
    loads[3].wait()
    loads[4].wait()
    loads[5].wait()

    def prepare(h, _):
        lanes = pl.ds(pl.multiple_of(h * HD, HD), HD)
        q_h = q_in[:, lanes]
        g_h = g_in[:, lanes]
        q_rows[lanes, :] = q_h
        g_rows[lanes, :] = g_h
        q_cols[:, lanes] = q_h.T
        g_cols[:, lanes] = g_h.T
        delta = jnp.sum(g_h.astype(F32) * o_in[:, lanes].astype(F32), axis=1, keepdims=True)
        delta_b[lanes, :] = jnp.broadcast_to(delta, (TOK, HD))
        norm = lse_in[pl.ds(h, 1), :]
        lse_b[lanes, :] = jnp.broadcast_to(norm, (HD, TOK)).T
        return 0

    lax.fori_loop(0, HEADS, prepare, 0, unroll=2)

    loads[6].wait()
    loads[7].wait()
    acts[...] = lax.dot_general(f_in[...], w_in[...], NT, preferred_element_type=F32)
    acts_down = remote(acts, acts_in.at[1], a_s.at[0], a_r.at[1], (lower, seq))
    acts_up = remote(acts, acts_in.at[0], a_s.at[1], a_r.at[0], (higher, seq))
    acts_down.start()
    acts_up.start()
    contrib_down = remote(contrib.at[0], contrib_in.at[1], c_s.at[0], c_r.at[1], (lower, seq))
    contrib_up = remote(contrib.at[1], contrib_in.at[0], c_s.at[1], c_r.at[0], (higher, seq))

    def gossip():
        acts_down.wait()
        acts_up.wait()
        columns = []
        for k in range(4):
            mine = acts[k : k + 1, :]
            source = jnp.concatenate(
                [mine - acts_in[0, k : k + 1, :], mine - acts_in[1, k : k + 1, :]], axis=0
            )
            vector = source
            for previous in columns:
                vector = vector - jnp.mean(source * previous, axis=1, keepdims=True) * previous
            columns.append(
                vector * lax.rsqrt(jnp.mean(vector * vector, axis=1, keepdims=True) + EPS)
            )
        basis = jnp.concatenate(
            [columns[k][e : e + 1, :] for e in range(2) for k in range(4)], axis=0
        )
        left_out[0, 0] = basis[0:4]
        left_out[0, 1] = basis[4:8]
        both = jnp.dot(basis.astype(BF16), w_in[...], preferred_element_type=F32)
        contrib[0] = both[0:4]
        contrib[1] = both[4:8]
        contrib_down.start()
        contrib_up.start()

    last = jnp.minimum(chip, SPAN)
    scale = HD ** (-0.5)
    dq_acc[...] = jnp.zeros_like(dq_acc)

    def part_copy(j):
        return remote(part.at[j, 1 - core], pin.at[j], pt_s.at[j], pt_r.at[j], dev(mate))

    def grad_copy(j):
        return remote(gsend.at[j], grecv.at[j], gr_s.at[j], gr_r.at[j], dev(seq - 2 * j))

    def finish(j):
        part_copy(j).wait_recv()
        total = part[j, core] + pin[j]

        @pl.when(j == 0)
        def _():
            own[...] = total

        @pl.when(j > 0)
        def _():
            gsend[j] = total.astype(BF16)
            grad_copy(j).start()

    def step(j, _):
        @pl.when(j < last)
        def _():
            kv_copy(j + 1).wait_recv()
            forward(j + 1).start()

        forward(j).wait_recv()
        query_pos = core * TOK + lax.broadcasted_iota(jnp.int32, (TOK, 2 * TOK), 0)
        gap = lax.broadcasted_iota(jnp.int32, (TOK, 2 * TOK), 1) - query_pos
        seen = (gap <= 2 * TOK * j) & (gap > 2 * TOK * j - WINDOW)
        bias[...] = jnp.where(seen, 0.0, -1e30)
        keys = kv_buf[j, :, :HD]
        vals = kv_buf[j, :, HD:]
        scores = lax.dot_general(q_rows[...], keys, NT, preferred_element_type=F32)
        prob_grad = lax.dot_general(g_rows[...], vals, NT, preferred_element_type=F32)
        norm = lse_b[...]
        delta = delta_b[...]
        logits = scores * scale - jnp.concatenate([norm, norm], axis=1)
        logits = logits.reshape(HEADS, TOK, 2 * TOK) + bias[...][None]
        probs = jnp.exp(logits).reshape(HEADS * TOK, 2 * TOK)
        probs_b = probs.astype(BF16)
        diff = prob_grad - jnp.concatenate([delta, delta], axis=1)
        score_grad = (scale * probs * diff).astype(BF16)
        dq_acc[...] += jnp.dot(score_grad, keys, preferred_element_type=F32)
        value_grad = jnp.dot(g_cols[...], probs_b, preferred_element_type=F32)
        key_grad = jnp.dot(q_cols[...], score_grad, preferred_element_type=F32)
        for c in range(2):
            cols = slice(c * TOK, (c + 1) * TOK)
            part[j, c, :HD, :] = key_grad[:, cols]
            part[j, c, HD:, :] = value_grad[:, cols]
        part_copy(j).start()

        @pl.when(j == 0)
        def _():
            gossip()

        @pl.when(j > 0)
        def _():
            finish(j - 1)

        return 0

    lax.fori_loop(0, last + 1, step, 0)
    finish(last)

    def dq_copy(h):
        lanes = pl.ds(pl.multiple_of(h * HD, HD), HD)
        return pltpu.make_async_copy(dq_acc.at[lanes, :], dq_out.at[0, :, lanes], dq_s.at[h])

    def dq_send(h, _):
        dq_copy(h).start()
        return 0

    lax.fori_loop(0, HEADS, dq_send, 0)

    def gather_grad(j, _):
        @pl.when(chip + j <= 15)
        def _():
            grad_copy(j).wait_recv()
            own[...] += grecv[j].astype(F32)

        return 0

    lax.fori_loop(1, SPAN + 1, gather_grad, 0)
    kg[me] = own[...].astype(BF16)

    def kg_copy(m):
        return remote(
            kg.at[me], kg.at[me], kg_s.at[m], kg_r.at[me],
            dev(16 * (m // 2) + 2 * zpos + m % 2),
        )

    def kg_wait(m):
        return remote(
            kg.at[m], kg.at[m], kg_s.at[m], kg_r.at[m],
            dev(16 * (m // 2) + 2 * zpos + m % 2),
        )

    for m in range(4):
        @pl.when(me != m)
        def _():
            kg_copy(m).start()

    kv_out[0] = own[...].T

    contrib_down.wait()
    contrib_up.wait()
    right_out[0, 0] = contrib[...] + contrib_in[...]

    def x_wait(n, _):
        m, i = n // 4, n % 4

        @pl.when(m == me)
        def _():
            x_copy(n, True).wait()

        @pl.when(m != me)
        def _():
            remote(
                x_slot(m, i), x_slot(m, i), x_s.at[n], x_r.at[n],
                dev(16 * (m // 2) + 2 * zpos + m % 2),
            ).wait_recv()
            x_copy(n, False).wait_send()

        return 0

    lax.fori_loop(0, 16, x_wait, 0)
    for m in range(4):
        @pl.when(me != m)
        def _():
            kg_wait(m).wait_recv()

    def p_copy(i, c):
        return remote(
            psend.at[i, c], precv.at[zpos], pr_s.at[i, c], pr_r.at[zpos],
            dev(16 * half + 2 * (2 * i + core) + c),
        )

    lhs = jnp.concatenate([kg[m] for m in range(4)], axis=1)
    for i in range(4):
        term = jnp.dot(lhs, x_all[:, i * ROWS : (i + 1) * ROWS], preferred_element_type=F32)
        term = term.astype(BF16).T
        psend[i, 0] = term[:HALF]
        psend[i, 1] = term[HALF:]
        for c in range(2):
            @pl.when(16 * half + 2 * (2 * i + core) + c != seq)
            def _():
                p_copy(i, c).start()

    proj_out[0] = jnp.zeros((HALF, 2 * HD), F32)

    def p_add(z, _):
        source = 16 * half + 2 * z + zpos % 2

        @pl.when(source == seq)
        def _():
            proj_out[0] += psend[zpos // 2, core].astype(F32)

        @pl.when(source != seq)
        def _():
            remote(
                precv.at[z], precv.at[z], pr_s.at[0, 0], pr_r.at[z], dev(source)
            ).wait_recv()
            proj_out[0] += precv[z].astype(F32)

        return 0

    lax.fori_loop(0, 8, p_add, 0)

    def drain_kv(j, _):
        @pl.when((j > 0) & (chip + j <= 15))
        def _():
            kv_copy(j).wait_send()

        @pl.when(j <= last)
        def _():
            forward(j).wait_send()
            part_copy(j).wait_send()

        @pl.when((j > 0) & (j <= last))
        def _():
            grad_copy(j).wait_send()

        return 0

    lax.fori_loop(0, SPAN + 1, drain_kv, 0)
    for m in range(4):
        @pl.when(me != m)
        def _():
            kg_copy(m).wait_send()
    for i in range(4):
        for c in range(2):
            @pl.when(16 * half + 2 * (2 * i + core) + c != seq)
            def _():
                p_copy(i, c).wait_send()

    def dq_wait(h, _):
        dq_copy(h).wait()
        return 0

    lax.fori_loop(0, HEADS, dq_wait, 0)


def on_device(*args):
    any_spec = pl.BlockSpec(memory_space=pl.ANY)
    vmem = pl.BlockSpec(memory_space=pltpu.VMEM)
    dma = pltpu.SemaphoreType.DMA
    n = SPAN + 1
    rows = HEADS * TOK
    return pl.pallas_call(
        kernel,
        out_shape=(
            jax.ShapeDtypeStruct((1, TOK, HEADS * HD), F32),
            jax.ShapeDtypeStruct((1, TOK, 2 * HD), F32),
            jax.ShapeDtypeStruct((1, HALF, 2 * HD), F32),
            jax.ShapeDtypeStruct((1, 2, 4, ROWS), F32),
            jax.ShapeDtypeStruct((1, 1, 2, 4, 6144), F32),
        ),
        in_specs=[any_spec] * 9,
        out_specs=(any_spec, vmem, vmem, vmem, vmem),
        scratch_shapes=[
            pltpu.VMEM((TOK, HEADS * HD), BF16),
            pltpu.VMEM((TOK, HEADS * HD), BF16),
            pltpu.VMEM((TOK, HEADS * HD), BF16),
            pltpu.VMEM((HEADS, TOK), F32),
            pltpu.VMEM((ROWS, 6144), BF16),
            pltpu.VMEM((4, 6144), BF16),
            pltpu.VMEM((rows, HD), BF16),
            pltpu.VMEM((rows, HD), BF16),
            pltpu.VMEM((HD, rows), BF16),
            pltpu.VMEM((HD, rows), BF16),
            pltpu.VMEM((rows, HD), F32),
            pltpu.VMEM((rows, HD), F32),
            pltpu.VMEM((rows, HD), F32),
            pltpu.VMEM((TOK, 2 * TOK), F32),
            pltpu.VMEM((n, 2 * TOK, 2 * HD), BF16),
            pltpu.VMEM((n, 2, 2 * HD, TOK), F32),
            pltpu.VMEM((n, 2 * HD, TOK), F32),
            pltpu.VMEM((n, 2 * HD, TOK), BF16),
            pltpu.VMEM((n, 2 * HD, TOK), BF16),
            pltpu.VMEM((2 * HD, TOK), F32),
            pltpu.VMEM((4 * TOK, 4 * ROWS), BF16),
            pltpu.VMEM((4, 2 * HD, TOK), BF16),
            pltpu.VMEM((4, 2, HALF, 2 * HD), BF16),
            pltpu.VMEM((8, HALF, 2 * HD), BF16),
            pltpu.VMEM((4, ROWS), F32),
            pltpu.VMEM((2, 4, ROWS), F32),
            pltpu.VMEM((2, 4, 6144), F32),
            pltpu.VMEM((2, 4, 6144), F32),
            dma((8,)),
            dma((n,)), dma((n,)), dma((n,)), dma((n,)), dma((n,)), dma((n,)), dma((n,)), dma((n,)),
            dma((16,)), dma((16,)), dma((4,)), dma((4,)), dma((4, 2)), dma((8,)),
            dma((2,)), dma((2,)), dma((2,)), dma((2,)), dma((HEADS,)),
        ],
        compiler_params=pltpu.CompilerParams(
            collective_id=0, has_side_effects=True, vmem_limit_bytes=62 * 1024 * 1024
        ),
        name="fused",
    )(*args)


def solution(mesh):
    return jax.shard_map(
        on_device,
        mesh=mesh,
        in_specs=(
            P("rep", "seq", None),
            P("rep", "seq", None),
            P("rep", "seq", None),
            P("rep", "seq", None),
            P("rep", "seq", None),
            P("rep", None, "seq"),
            P("rep", "seq", None),
            P("rep", "seq", None),
            P("seq", None, None),
        ),
        out_specs=(
            P("rep", "seq", None),
            P("rep", "seq", None),
            P("rep", "seq", None),
            P("rep", None, None, "seq"),
            P("rep", "seq", None, None, None),
        ),
        check_vma=False,
    )
```

```python
import functools

import jax
import jax.numpy as jnp
from jax import lax
from jax.experimental import pallas as pl
from jax.experimental.pallas import tpu as pltpu
from jax.sharding import PartitionSpec as P

MESH = pl.DeviceIdType.MESH
F32 = jnp.float32
BF16 = jnp.bfloat16
EPS = 1e-06
NT = (((1,), (1,)), ((), ()))

HD = 128
HEADS = 24
TOK = 128
SPAN = 8
ROWS = 384
HALF = 192
WINDOW = 2048
ORDERS = ((1, 7, 3, 6, 5, 4, 2, 8), (1, 8, 7, 6, 3, 5, 4, 2))
PIECES = 4
PIECE = ROWS // PIECES


def kernel(
    q_hbm, k_hbm, v_hbm, o_hbm, g_hbm, lse_hbm, x_hbm, w_hbm, f_hbm,
    dq_acc, kv_out, proj_out, left_out, right_out,
    q_in, g_in, o_in, lse_in, w_in, f_in,
    q_rows, g_rows, q_cols, g_cols, lse_b, delta_b, bias,
    kv_buf, part, pin, gsend, grecv, own, x_all, kg,
    term, chain_out, chain_in, final_in, mate_in,
    acts, acts_in, contrib, contrib_in,
    load_sem, kv_s, kv_r, fw_s, fw_r, pt_s, pt_r, gr_s, gr_r,
    x_s, x_r, kg_s, kg_r, ch_s, ch_r, fi_r, mt_s, mt_r, a_s, a_r, c_s, c_r,
):
    rep = lax.axis_index("rep")
    seq = lax.axis_index("seq")
    core = seq % 2
    chip = seq // 2
    half = chip // 8
    zpos = chip % 8
    mate = seq + 1 - 2 * core
    lower = (rep + 7) % 8
    higher = (rep + 1) % 8
    me = 2 * half + core

    def dev(s):
        return (rep, s)

    def remote(src, dst, ss, rs, target):
        return pltpu.make_async_remote_copy(
            src_ref=src, dst_ref=dst, send_sem=ss, recv_sem=rs,
            device_id=target, device_id_type=MESH,
        )

    barrier = pltpu.get_barrier_semaphore()

    def greet(i, _):
        pl.semaphore_signal(barrier, inc=1, device_id=dev((seq + i) % 32), device_id_type=MESH)
        return 0

    own_rows = pl.ds(pl.multiple_of(core * TOK, TOK), TOK)
    loads = [
        pltpu.make_async_copy(k_hbm.at[0], kv_buf.at[0, own_rows, pl.ds(0, HD)], load_sem.at[0]),
        pltpu.make_async_copy(v_hbm.at[0], kv_buf.at[0, own_rows, pl.ds(HD, HD)], load_sem.at[1]),
        pltpu.make_async_copy(q_hbm.at[0], q_in, load_sem.at[2]),
        pltpu.make_async_copy(g_hbm.at[0], g_in, load_sem.at[3]),
        pltpu.make_async_copy(o_hbm.at[0], o_in, load_sem.at[4]),
        pltpu.make_async_copy(lse_hbm.at[0], lse_in, load_sem.at[5]),
        pltpu.make_async_copy(f_hbm.at[0], f_in, load_sem.at[6]),
        pltpu.make_async_copy(w_hbm.at[0], w_in, load_sem.at[7]),
    ]
    for load in loads:
        load.start()
    lax.fori_loop(1, 32, greet, 0)
    for other in (lower, higher):
        pl.semaphore_signal(barrier, inc=1, device_id=(other, seq), device_id_type=MESH)

    pl.semaphore_wait(barrier, 33)

    loads[0].wait()
    loads[1].wait()

    def kv_copy(j):
        return remote(
            kv_buf.at[0, own_rows, :], kv_buf.at[j, own_rows, :],
            kv_s.at[j], kv_r.at[j], dev(seq + 2 * j),
        )

    def forward(j):
        return remote(
            kv_buf.at[j, own_rows, :], kv_buf.at[j, own_rows, :],
            fw_s.at[j], fw_r.at[j], dev(mate),
        )

    forward(0).start()

    def kv_send(j):
        @pl.when(chip + j <= 15)
        def _():
            kv_copy(j).start()

    for j in (1, 8, 7, 6, 5):
        kv_send(j)

    def x_slot(m, i):
        return x_all.at[
            pl.ds(pl.multiple_of(m * TOK, TOK), TOK), pl.ds(pl.multiple_of(i * ROWS, ROWS), ROWS)
        ]

    def x_copy(n, local):
        m, i = n // 4, n % 4
        block = 8 * (m // 2) + 2 * i + m % 2
        src = x_hbm.at[0, :, pl.ds(pl.multiple_of(block * ROWS, ROWS), ROWS)]
        if local:
            return pltpu.make_async_copy(src, x_slot(me, i), x_r.at[n])
        return remote(
            src, x_slot(me, i), x_s.at[n], x_r.at[4 * me + i],
            dev(16 * (m // 2) + 2 * zpos + m % 2),
        )

    def x_send(n, _):
        @pl.when(n // 4 == me)
        def _():
            x_copy(n, True).start()

        @pl.when(n // 4 != me)
        def _():
            x_copy(n, False).start()

        return 0

    loads[2].wait()
    loads[3].wait()
    loads[4].wait()
    loads[5].wait()

    def prepare(h, _):
        lanes = pl.ds(pl.multiple_of(h * HD, HD), HD)
        q_h = q_in[:, lanes]
        g_h = g_in[:, lanes]
        q_rows[lanes, :] = q_h
        g_rows[lanes, :] = g_h
        q_cols[:, lanes] = q_h.T
        g_cols[:, lanes] = g_h.T
        delta = jnp.sum(g_h.astype(F32) * o_in[:, lanes].astype(F32), axis=1, keepdims=True)
        delta_b[lanes, :] = jnp.broadcast_to(delta, (TOK, HD))
        norm = lse_in[pl.ds(h, 1), :]
        lse_b[lanes, :] = jnp.broadcast_to(norm, (HD, TOK)).T
        return 0

    lax.fori_loop(0, HEADS, prepare, 0, unroll=2)
    kv_send(3)
    lax.fori_loop(0, 16, x_send, 0)

    acts_down = remote(acts, acts_in.at[1], a_s.at[0], a_r.at[1], (lower, seq))
    acts_up = remote(acts, acts_in.at[0], a_s.at[1], a_r.at[0], (higher, seq))
    contrib_down = remote(contrib.at[0], contrib_in.at[1], c_s.at[0], c_r.at[1], (lower, seq))
    contrib_up = remote(contrib.at[1], contrib_in.at[0], c_s.at[1], c_r.at[0], (higher, seq))

    def gossip():
        acts_down.wait()
        acts_up.wait()
        columns = []
        for k in range(4):
            mine = acts[k : k + 1, :]
            source = jnp.concatenate(
                [mine - acts_in[0, k : k + 1, :], mine - acts_in[1, k : k + 1, :]], axis=0
            )
            vector = source
            for previous in columns:
                vector = vector - jnp.mean(source * previous, axis=1, keepdims=True) * previous
            columns.append(
                vector * lax.rsqrt(jnp.mean(vector * vector, axis=1, keepdims=True) + EPS)
            )
        basis = jnp.concatenate(
            [columns[k][e : e + 1, :] for e in range(2) for k in range(4)], axis=0
        )
        left_out[0, 0] = basis[0:4]
        left_out[0, 1] = basis[4:8]
        both = jnp.dot(basis.astype(BF16), w_in[...], preferred_element_type=F32)
        contrib[0] = both[0:4]
        contrib[1] = both[4:8]
        contrib_down.start()
        contrib_up.start()

    last = jnp.minimum(chip, SPAN)

    def block_at(n):
        block, before = 0, 1
        for low, high in zip(*ORDERS):
            j = jnp.where(half == 0, low, high)
            held = j <= last
            block = jnp.where(held & (before == n), j, block)
            before = before + jnp.where(held, 1, 0)
        return block

    scale = HD ** (-0.5)
    dq_acc[...] = jnp.zeros_like(dq_acc)

    def part_copy(j):
        return remote(part.at[j, 1 - core], pin.at[j], pt_s.at[j], pt_r.at[j], dev(mate))

    def grad_copy(j):
        return remote(gsend.at[j], grecv.at[j], gr_s.at[j], gr_r.at[j], dev(seq - 2 * j))

    def finish(j):
        part_copy(j).wait_recv()
        total = part[j, core] + pin[j]

        @pl.when(j == 0)
        def _():
            own[...] = total

        @pl.when(j > 0)
        def _():
            gsend[j] = total.astype(BF16)
            grad_copy(j).start()

    def pass_on(n):
        @pl.when(n <= last)
        def _():
            kv_copy(block_at(n)).wait_recv()
            forward(block_at(n)).start()

    def step(n, _):
        j = block_at(n)
        pass_on(n + 1)
        forward(j).wait_recv()

        @pl.when(n == jnp.minimum(1, last))
        def _():
            kv_send(4)

        @pl.when(n == jnp.minimum(2, last))
        def _():
            kv_send(2)

        query_pos = core * TOK + lax.broadcasted_iota(jnp.int32, (TOK, 2 * TOK), 0)
        gap = lax.broadcasted_iota(jnp.int32, (TOK, 2 * TOK), 1) - query_pos
        seen = (gap <= 2 * TOK * j) & (gap > 2 * TOK * j - WINDOW)
        bias[...] = jnp.where(seen, 0.0, -1e30)
        keys = kv_buf[j, :, :HD]
        vals = kv_buf[j, :, HD:]
        scores = lax.dot_general(q_rows[...], keys, NT, preferred_element_type=F32)
        prob_grad = lax.dot_general(g_rows[...], vals, NT, preferred_element_type=F32)
        norm = lse_b[...]
        delta = delta_b[...]
        logits = scores * scale - jnp.concatenate([norm, norm], axis=1)
        logits = logits.reshape(HEADS, TOK, 2 * TOK) + bias[...][None]
        probs = jnp.exp(logits).reshape(HEADS * TOK, 2 * TOK)
        probs_b = probs.astype(BF16)
        diff = prob_grad - jnp.concatenate([delta, delta], axis=1)
        score_grad = (scale * probs * diff).astype(BF16)
        dq_acc[...] += jnp.dot(score_grad, keys, preferred_element_type=F32)
        value_grad = jnp.dot(g_cols[...], probs_b, preferred_element_type=F32)
        key_grad = jnp.dot(q_cols[...], score_grad, preferred_element_type=F32)
        for c in range(2):
            cols = slice(c * TOK, (c + 1) * TOK)
            part[j, c, :HD, :] = key_grad[:, cols]
            part[j, c, HD:, :] = value_grad[:, cols]
        part_copy(j).start()

        @pl.when(n > 0)
        def _():
            finish(block_at(n - 1))

        return 0

    lax.fori_loop(0, last + 1, step, 0)
    finish(block_at(last))

    loads[6].wait()
    loads[7].wait()
    acts[...] = lax.dot_general(f_in[...], w_in[...], NT, preferred_element_type=F32)
    acts_down.start()
    acts_up.start()

    def gather_grad(j, _):
        @pl.when(chip + j <= 15)
        def _():
            grad_copy(j).wait_recv()
            own[...] += grecv[j].astype(F32)

        return 0

    lax.fori_loop(1, SPAN + 1, gather_grad, 0)
    kg[me] = own[...].astype(BF16)

    mate_m = 2 * half + 1 - core
    over_m = 2 * (1 - half) + core
    cross_m = 2 * (1 - half) + 1 - core
    over = 16 * (1 - half) + 2 * zpos + core

    def kg_copy(m, k, target):
        return remote(kg.at[m], kg.at[m], kg_s.at[k], kg_r.at[m], dev(target))

    kg_over = kg_copy(me, 0, over)
    kg_mate = kg_copy(me, 1, mate)
    kg_pass = kg_copy(over_m, 2, mate)
    kg_over.start()
    kg_mate.start()

    kv_out[0] = own[...].T
    gossip()

    def x_wait(n, _):
        m, i = n // 4, n % 4

        @pl.when(m == me)
        def _():
            x_copy(n, True).wait()

        @pl.when(m != me)
        def _():
            remote(
                x_slot(m, i), x_slot(m, i), x_s.at[n], x_r.at[n],
                dev(16 * (m // 2) + 2 * zpos + m % 2),
            ).wait_recv()
            x_copy(n, False).wait_send()

        return 0

    lax.fori_loop(0, 16, x_wait, 0)
    kg_copy(over_m, 2, mate).wait_recv()
    kg_pass.start()
    kg_copy(mate_m, 1, mate).wait_recv()
    kg_copy(cross_m, 2, mate).wait_recv()

    even = zpos % 2 == core
    lhs = jnp.concatenate([kg[m] for m in range(4)], axis=1)

    def place(z, c):
        return dev(16 * half + 2 * (z % 8) + c)

    def product(t):
        ahead = jnp.where(even, (4, 6, 2, 0)[t], (5, 3, 7, 1)[t])
        block = ((zpos + 8 - ahead) % 8) // 2
        cols = pl.ds(pl.multiple_of(block * ROWS, ROWS), ROWS)
        term[...] = jnp.dot(lhs, x_all[:, cols], preferred_element_type=F32).T

    def hop(t, u, z):
        return remote(
            chain_out.at[t, u], chain_in.at[t, u], ch_s.at[t, u], ch_r.at[t, u], place(z, core)
        )

    def last_hop(t, u, side):
        return remote(
            chain_out.at[t, u], final_in.at[side, u % (PIECES // 2)],
            ch_s.at[t, u], fi_r.at[side, u % (PIECES // 2)],
            place(zpos + 9 - 2 * (1 - side), u // (PIECES // 2)),
        )

    def mate_hop():
        rows = pl.ds(pl.multiple_of((1 - core) * HALF, HALF), HALF)
        return remote(term.at[rows, :], mate_in, mt_s, mt_r, dev(mate))

    towards = jnp.where(even, 7, 1)
    backwards = jnp.where(even, 1, 7)
    for t in range(4):
        product(t)
        for u in range(PIECES):
            rows = slice(u * PIECE, (u + 1) * PIECE)
            if t == 0:
                chain_out[0, u] = term[rows, :].astype(BF16)
                hop(0, u, zpos + towards).start()
                continue
            if t < 3:
                hop(t - 1, u, zpos + backwards).wait_recv()
                chain_out[t, u] = (term[rows, :] + chain_in[t - 1, u].astype(F32)).astype(BF16)
            if t == 1:
                hop(1, u, zpos + backwards).start()
            if t == 2:
                @pl.when(even)
                def _():
                    hop(2, u, zpos + 7).start()

                @pl.when(jnp.logical_not(even))
                def _():
                    last_hop(2, u, 1).start()
            if t == 3:
                @pl.when(jnp.logical_not(even))
                def _():
                    hop(2, u, zpos + 1).wait_recv()
                    chain_out[3, u] = (term[rows, :] + chain_in[2, u].astype(F32)).astype(BF16)
                    last_hop(3, u, 0).start()

    own_half = pl.ds(pl.multiple_of(core * HALF, HALF), HALF)

    @pl.when(even)
    def _():
        mate_hop().start()
        proj_out[0] = term[own_half, :]

    contrib_down.wait()
    contrib_up.wait()
    right_out[0, 0] = contrib[...] + contrib_in[...]

    @pl.when(jnp.logical_not(even))
    def _():
        mate_hop().wait_recv()
        proj_out[0] = mate_in[...]

    for side in (1, 0):
        for v in range(PIECES // 2):
            rows = slice(v * PIECE, (v + 1) * PIECE)
            last_hop(2, v, side).wait_recv()
            proj_out[0, rows, :] += final_in[side, v].astype(F32)

    def drain_kv(j, _):
        @pl.when((j > 0) & (chip + j <= 15))
        def _():
            kv_copy(j).wait_send()

        @pl.when(j <= last)
        def _():
            forward(j).wait_send()
            part_copy(j).wait_send()

        @pl.when((j > 0) & (j <= last))
        def _():
            grad_copy(j).wait_send()

        return 0

    lax.fori_loop(0, SPAN + 1, drain_kv, 0)
    kg_over.wait_send()
    kg_mate.wait_send()
    kg_pass.wait_send()
    for u in range(PIECES):
        for t in range(3):
            hop(t, u, zpos + 1).wait_send()

        @pl.when(jnp.logical_not(even))
        def _():
            last_hop(3, u, 0).wait_send()

    @pl.when(even)
    def _():
        mate_hop().wait_send()


def emit(dq, kv, proj, left, right, dq_out, kv_out, proj_out, left_out, right_out, sem, head_sem):
    copies = [
        pltpu.make_async_copy(src, dst, sem.at[k])
        for k, (src, dst) in enumerate(
            ((kv, kv_out), (proj, proj_out), (left, left_out), (right, right_out))
        )
    ]
    for h in range(HEADS):
        lanes = slice(h * HD, (h + 1) * HD)
        copies.append(
            pltpu.make_async_copy(dq.at[lanes, :], dq_out.at[0, :, lanes], head_sem.at[h])
        )
    for copy in copies:
        copy.start()
    for copy in copies:
        copy.wait()


def on_device(*args):
    any_spec = pl.BlockSpec(memory_space=pl.ANY)
    vmem = pl.BlockSpec(memory_space=pltpu.VMEM)
    dma = pltpu.SemaphoreType.DMA
    n = SPAN + 1
    rows = HEADS * TOK
    results = pl.pallas_call(
        kernel,
        out_shape=(
            pltpu.VMEM((rows, HD), F32),
            pltpu.VMEM((1, TOK, 2 * HD), F32),
            pltpu.VMEM((1, HALF, 2 * HD), F32),
            pltpu.VMEM((1, 2, 4, ROWS), F32),
            pltpu.VMEM((1, 1, 2, 4, 6144), F32),
        ),
        in_specs=[any_spec] * 9,
        out_specs=(vmem,) * 5,
        scratch_shapes=[
            pltpu.VMEM((TOK, HEADS * HD), BF16),
            pltpu.VMEM((TOK, HEADS * HD), BF16),
            pltpu.VMEM((TOK, HEADS * HD), BF16),
            pltpu.VMEM((HEADS, TOK), F32),
            pltpu.VMEM((ROWS, 6144), BF16),
            pltpu.VMEM((4, 6144), BF16),
            pltpu.VMEM((rows, HD), BF16),
            pltpu.VMEM((rows, HD), BF16),
            pltpu.VMEM((HD, rows), BF16),
            pltpu.VMEM((HD, rows), BF16),
            pltpu.VMEM((rows, HD), F32),
            pltpu.VMEM((rows, HD), F32),
            pltpu.VMEM((TOK, 2 * TOK), F32),
            pltpu.VMEM((n, 2 * TOK, 2 * HD), BF16),
            pltpu.VMEM((n, 2, 2 * HD, TOK), F32),
            pltpu.VMEM((n, 2 * HD, TOK), F32),
            pltpu.VMEM((n, 2 * HD, TOK), BF16),
            pltpu.VMEM((n, 2 * HD, TOK), BF16),
            pltpu.VMEM((2 * HD, TOK), F32),
            pltpu.VMEM((4 * TOK, 4 * ROWS), BF16),
            pltpu.VMEM((4, 2 * HD, TOK), BF16),
            pltpu.VMEM((ROWS, 2 * HD), F32),
            pltpu.VMEM((4, PIECES, PIECE, 2 * HD), BF16),
            pltpu.VMEM((3, PIECES, PIECE, 2 * HD), BF16),
            pltpu.VMEM((2, PIECES // 2, PIECE, 2 * HD), BF16),
            pltpu.VMEM((HALF, 2 * HD), F32),
            pltpu.VMEM((4, ROWS), F32),
            pltpu.VMEM((2, 4, ROWS), F32),
            pltpu.VMEM((2, 4, 6144), F32),
            pltpu.VMEM((2, 4, 6144), F32),
            dma((8,)),
            dma((n,)), dma((n,)), dma((n,)), dma((n,)), dma((n,)), dma((n,)), dma((n,)), dma((n,)),
            dma((16,)), dma((16,)), dma((3,)), dma((4,)),
            dma((4, PIECES)), dma((3, PIECES)), dma((2, PIECES // 2)), dma, dma,
            dma((2,)), dma((2,)), dma((2,)), dma((2,)),
        ],
        compiler_params=pltpu.CompilerParams(
            collective_id=0, has_side_effects=True, vmem_limit_bytes=56 * 1024 * 1024
        ),
        name="fused",
    )(*args)
    return pl.pallas_call(
        emit,
        out_shape=(
            jax.ShapeDtypeStruct((1, TOK, HEADS * HD), F32),
            jax.ShapeDtypeStruct((1, TOK, 2 * HD), F32),
            jax.ShapeDtypeStruct((1, HALF, 2 * HD), F32),
            jax.ShapeDtypeStruct((1, 2, 4, ROWS), F32),
            jax.ShapeDtypeStruct((1, 1, 2, 4, 6144), F32),
        ),
        in_specs=[vmem] * 5,
        out_specs=(any_spec,) * 5,
        scratch_shapes=[dma((4,)), dma((HEADS,))],
        compiler_params=pltpu.CompilerParams(vmem_limit_bytes=4 * 1024 * 1024),
        name="emit",
    )(*results)


def solution(mesh):
    return jax.shard_map(
        on_device,
        mesh=mesh,
        in_specs=(
            P("rep", "seq", None),
            P("rep", "seq", None),
            P("rep", "seq", None),
            P("rep", "seq", None),
            P("rep", "seq", None),
            P("rep", None, "seq"),
            P("rep", "seq", None),
            P("rep", "seq", None),
            P("seq", None, None),
        ),
        out_specs=(
            P("rep", "seq", None),
            P("rep", "seq", None),
            P("rep", "seq", None),
            P("rep", None, None, "seq"),
            P("rep", "seq", None, None, None),
        ),
        check_vma=False,
    )
```

```python
import functools

import jax
import jax.numpy as jnp
from jax import lax
from jax.experimental import pallas as pl
from jax.experimental.pallas import tpu as pltpu
from jax.sharding import PartitionSpec as P

MESH = pl.DeviceIdType.MESH
F32 = jnp.float32
BF16 = jnp.bfloat16
EPS = 1e-06
NT = (((1,), (1,)), ((), ()))

HD = 128
HEADS = 24
TOK = 128
SPAN = 8
ROWS = 384
HALF = 192
WINDOW = 2048
ORDERS = ((5, 3, 4, 6, 7, 2, 1, 8), (8, 5, 3, 4, 6, 2, 7, 1))
PIECES = 6
PIECE = ROWS // PIECES


def kernel(
    q_hbm, k_hbm, v_hbm, o_hbm, g_hbm, lse_hbm, x_hbm, w_hbm, f_hbm,
    dq_acc, kv_out, proj_out, left_out, right_out,
    q_in, g_in, o_in, lse_in, w_in, f_in,
    q_rows, g_rows, q_cols, g_cols, lse_b, delta_b, bias,
    kv_buf, part, pin, gsend, grecv, own, x_all, kg,
    term, chain_out, chain_in, final_in, mate_in,
    acts, acts_in, contrib, contrib_in,
    load_sem, kv_s, kv_r, sp_s, fw_s, fw_r, pt_s, pt_r, gr_s, gr_r,
    x_s, x_r, kg_s, kg_r, ch_s, ch_r, fi_r, mt_s, mt_r, a_s, a_r, c_s, c_r,
):
    rep = lax.axis_index("rep")
    seq = lax.axis_index("seq")
    core = seq % 2
    chip = seq // 2
    half = chip // 8
    zpos = chip % 8
    mate = seq + 1 - 2 * core
    lower = (rep + 7) % 8
    higher = (rep + 1) % 8
    me = 2 * half + core

    def dev(s):
        return (rep, s)

    def remote(src, dst, ss, rs, target):
        return pltpu.make_async_remote_copy(
            src_ref=src, dst_ref=dst, send_sem=ss, recv_sem=rs,
            device_id=target, device_id_type=MESH,
        )

    barrier = pltpu.get_barrier_semaphore()

    def greet(i, _):
        pl.semaphore_signal(barrier, inc=1, device_id=dev((seq + i) % 32), device_id_type=MESH)
        return 0

    own_rows = pl.ds(pl.multiple_of(core * TOK, TOK), TOK)
    loads = [
        pltpu.make_async_copy(k_hbm.at[0], kv_buf.at[0, own_rows, pl.ds(0, HD)], load_sem.at[0]),
        pltpu.make_async_copy(v_hbm.at[0], kv_buf.at[0, own_rows, pl.ds(HD, HD)], load_sem.at[1]),
        pltpu.make_async_copy(q_hbm.at[0], q_in, load_sem.at[2]),
        pltpu.make_async_copy(g_hbm.at[0], g_in, load_sem.at[3]),
        pltpu.make_async_copy(o_hbm.at[0], o_in, load_sem.at[4]),
        pltpu.make_async_copy(lse_hbm.at[0], lse_in, load_sem.at[5]),
        pltpu.make_async_copy(f_hbm.at[0], f_in, load_sem.at[6]),
        pltpu.make_async_copy(w_hbm.at[0], w_in, load_sem.at[7]),
    ]
    for load in loads:
        load.start()
    lax.fori_loop(1, 32, greet, 0)
    for other in (lower, higher):
        pl.semaphore_signal(barrier, inc=1, device_id=(other, seq), device_id_type=MESH)

    pl.semaphore_wait(barrier, 33)

    loads[0].wait()
    loads[1].wait()

    def kv_copy(j):
        return remote(
            kv_buf.at[0, own_rows, :], kv_buf.at[j, own_rows, :],
            kv_s.at[j], kv_r.at[j], dev(seq + 2 * j),
        )

    def forward(j):
        return remote(
            kv_buf.at[j, own_rows, :], kv_buf.at[j, own_rows, :],
            fw_s.at[j], fw_r.at[j], dev(mate),
        )

    forward(0).start()

    def kv_send(j):
        held = chip + j <= 15
        if j in (6, 7):
            held = zpos + j <= 7

        @pl.when(held)
        def _():
            kv_copy(j).start()

    def spread(j):
        return remote(
            kv_buf.at[SPAN, own_rows, :], kv_buf.at[j, own_rows, :],
            sp_s.at[j - 5], kv_r.at[j], dev(seq + 2 * (j - SPAN)),
        )

    for j in (8, 5, 3, 4, 6, 7, 2, 1):
        kv_send(j)

    def x_slot(m, i):
        return x_all.at[
            pl.ds(pl.multiple_of(m * TOK, TOK), TOK), pl.ds(pl.multiple_of(i * ROWS, ROWS), ROWS)
        ]

    def x_copy(n, local):
        m, i = n // 4, n % 4
        block = 8 * (m // 2) + 2 * i + m % 2
        src = x_hbm.at[0, :, pl.ds(pl.multiple_of(block * ROWS, ROWS), ROWS)]
        if local:
            return pltpu.make_async_copy(src, x_slot(me, i), x_r.at[n])
        return remote(
            src, x_slot(me, i), x_s.at[n], x_r.at[4 * me + i],
            dev(16 * (m // 2) + 2 * zpos + m % 2),
        )

    def x_send(n, _):
        @pl.when(n // 4 == me)
        def _():
            x_copy(n, True).start()

        @pl.when(n // 4 != me)
        def _():
            x_copy(n, False).start()

        return 0

    loads[2].wait()
    loads[3].wait()
    loads[4].wait()
    loads[5].wait()

    def prepare(h, _):
        lanes = pl.ds(pl.multiple_of(h * HD, HD), HD)
        q_h = q_in[:, lanes]
        g_h = g_in[:, lanes]
        q_rows[lanes, :] = q_h
        g_rows[lanes, :] = g_h
        q_cols[:, lanes] = q_h.T
        g_cols[:, lanes] = g_h.T
        delta = jnp.sum(g_h.astype(F32) * o_in[:, lanes].astype(F32), axis=1, keepdims=True)
        delta_b[lanes, :] = jnp.broadcast_to(delta, (TOK, HD))
        norm = lse_in[pl.ds(h, 1), :]
        lse_b[lanes, :] = jnp.broadcast_to(norm, (HD, TOK)).T
        return 0

    lax.fori_loop(0, HEADS, prepare, 0, unroll=2)
    lax.fori_loop(0, 16, x_send, 0)

    acts_down = remote(acts, acts_in.at[1], a_s.at[0], a_r.at[1], (lower, seq))
    acts_up = remote(acts, acts_in.at[0], a_s.at[1], a_r.at[0], (higher, seq))
    contrib_down = remote(contrib.at[0], contrib_in.at[1], c_s.at[0], c_r.at[1], (lower, seq))
    contrib_up = remote(contrib.at[1], contrib_in.at[0], c_s.at[1], c_r.at[0], (higher, seq))

    def gossip():
        acts_down.wait()
        acts_up.wait()
        columns = []
        for k in range(4):
            mine = acts[k : k + 1, :]
            source = jnp.concatenate(
                [mine - acts_in[0, k : k + 1, :], mine - acts_in[1, k : k + 1, :]], axis=0
            )
            vector = source
            for previous in columns:
                vector = vector - jnp.mean(source * previous, axis=1, keepdims=True) * previous
            columns.append(
                vector * lax.rsqrt(jnp.mean(vector * vector, axis=1, keepdims=True) + EPS)
            )
        basis = jnp.concatenate(
            [columns[k][e : e + 1, :] for e in range(2) for k in range(4)], axis=0
        )
        left_out[0, 0] = basis[0:4]
        left_out[0, 1] = basis[4:8]
        both = jnp.dot(basis.astype(BF16), w_in[...], preferred_element_type=F32)
        contrib[0] = both[0:4]
        contrib[1] = both[4:8]
        contrib_down.start()
        contrib_up.start()

    last = jnp.minimum(chip, SPAN)

    def block_at(n):
        block, before = 0, 1
        for low, high in zip(*ORDERS):
            j = jnp.where(half == 0, low, high)
            held = j <= last
            block = jnp.where(held & (before == n), j, block)
            before = before + jnp.where(held, 1, 0)
        return block

    scale = HD ** (-0.5)
    dq_acc[...] = jnp.zeros_like(dq_acc)

    def part_copy(j):
        return remote(part.at[j, 1 - core], pin.at[j], pt_s.at[j], pt_r.at[j], dev(mate))

    def grad_copy(j):
        return remote(gsend.at[j], grecv.at[j], gr_s.at[j], gr_r.at[j], dev(seq - 2 * j))

    def finish(j):
        part_copy(j).wait_recv()
        total = part[j, core] + pin[j]

        @pl.when(j == 0)
        def _():
            own[...] = total

        @pl.when(j > 0)
        def _():
            gsend[j] = total.astype(BF16)
            grad_copy(j).start()

    def pass_on(n):
        @pl.when(n <= last)
        def _():
            kv_copy(block_at(n)).wait_recv()
            forward(block_at(n)).start()

        @pl.when((half == 1) & (n == 1))
        def _():
            for j in (6, 7):
                @pl.when(zpos + j >= SPAN)
                def _():
                    spread(j).start()

    def step(n, _):
        j = block_at(n)
        pass_on(n + 1)
        forward(j).wait_recv()

        query_pos = core * TOK + lax.broadcasted_iota(jnp.int32, (TOK, 2 * TOK), 0)
        gap = lax.broadcasted_iota(jnp.int32, (TOK, 2 * TOK), 1) - query_pos
        seen = (gap <= 2 * TOK * j) & (gap > 2 * TOK * j - WINDOW)
        bias[...] = jnp.where(seen, 0.0, -1e30)
        keys = kv_buf[j, :, :HD]
        vals = kv_buf[j, :, HD:]
        scores = lax.dot_general(q_rows[...], keys, NT, preferred_element_type=F32)
        prob_grad = lax.dot_general(g_rows[...], vals, NT, preferred_element_type=F32)
        norm = lse_b[...]
        delta = delta_b[...]
        logits = scores * scale - jnp.concatenate([norm, norm], axis=1)
        logits = logits.reshape(HEADS, TOK, 2 * TOK) + bias[...][None]
        probs = jnp.exp(logits).reshape(HEADS * TOK, 2 * TOK)
        probs_b = probs.astype(BF16)
        diff = prob_grad - jnp.concatenate([delta, delta], axis=1)
        score_grad = (scale * probs * diff).astype(BF16)
        dq_acc[...] += jnp.dot(score_grad, keys, preferred_element_type=F32)
        value_grad = jnp.dot(g_cols[...], probs_b, preferred_element_type=F32)
        key_grad = jnp.dot(q_cols[...], score_grad, preferred_element_type=F32)
        for c in range(2):
            cols = slice(c * TOK, (c + 1) * TOK)
            part[j, c, :HD, :] = key_grad[:, cols]
            part[j, c, HD:, :] = value_grad[:, cols]
        part_copy(j).start()

        @pl.when(n > 0)
        def _():
            finish(block_at(n - 1))

        return 0

    lax.fori_loop(0, last + 1, step, 0)
    finish(block_at(last))

    loads[6].wait()
    loads[7].wait()
    acts[...] = lax.dot_general(f_in[...], w_in[...], NT, preferred_element_type=F32)
    acts_down.start()
    acts_up.start()

    def gather_grad(j, _):
        @pl.when(chip + j <= 15)
        def _():
            grad_copy(j).wait_recv()
            own[...] += grecv[j].astype(F32)

        return 0

    lax.fori_loop(1, SPAN + 1, gather_grad, 0)
    kg[me] = own[...].astype(BF16)

    mate_m = 2 * half + 1 - core
    over_m = 2 * (1 - half) + core
    cross_m = 2 * (1 - half) + 1 - core
    over = 16 * (1 - half) + 2 * zpos + core

    def kg_copy(m, k, target):
        return remote(kg.at[m], kg.at[m], kg_s.at[k], kg_r.at[m], dev(target))

    kg_over = kg_copy(me, 0, over)
    kg_mate = kg_copy(me, 1, mate)
    kg_pass = kg_copy(over_m, 2, mate)
    kg_over.start()
    kg_mate.start()

    kv_out[0] = own[...].T
    gossip()

    def x_wait(n, _):
        m, i = n // 4, n % 4

        @pl.when(m == me)
        def _():
            x_copy(n, True).wait()

        @pl.when(m != me)
        def _():
            remote(
                x_slot(m, i), x_slot(m, i), x_s.at[n], x_r.at[n],
                dev(16 * (m // 2) + 2 * zpos + m % 2),
            ).wait_recv()
            x_copy(n, False).wait_send()

        return 0

    lax.fori_loop(0, 16, x_wait, 0)
    kg_copy(over_m, 2, mate).wait_recv()
    kg_pass.start()
    kg_copy(mate_m, 1, mate).wait_recv()
    kg_copy(cross_m, 2, mate).wait_recv()

    even = zpos % 2 == core
    lhs = jnp.concatenate([kg[m] for m in range(4)], axis=1)

    def place(z, c):
        return dev(16 * half + 2 * (z % 8) + c)

    def product(t):
        ahead = jnp.where(even, (4, 6, 2, 0)[t], (5, 3, 7, 1)[t])
        block = ((zpos + 8 - ahead) % 8) // 2
        cols = pl.ds(pl.multiple_of(block * ROWS, ROWS), ROWS)
        term[...] = jnp.dot(lhs, x_all[:, cols], preferred_element_type=F32).T

    def hop(t, u, z):
        return remote(
            chain_out.at[t, u], chain_in.at[t, u], ch_s.at[t, u], ch_r.at[t, u], place(z, core)
        )

    def last_hop(t, u, side):
        return remote(
            chain_out.at[t, u], final_in.at[side, u % (PIECES // 2)],
            ch_s.at[t, u], fi_r.at[side, u % (PIECES // 2)],
            place(zpos + 9 - 2 * (1 - side), u // (PIECES // 2)),
        )

    def mate_hop():
        rows = pl.ds(pl.multiple_of((1 - core) * HALF, HALF), HALF)
        return remote(term.at[rows, :], mate_in, mt_s, mt_r, dev(mate))

    towards = jnp.where(even, 7, 1)
    backwards = jnp.where(even, 1, 7)
    for t in range(4):
        product(t)
        for u in range(PIECES):
            rows = slice(u * PIECE, (u + 1) * PIECE)
            if t == 0:
                chain_out[0, u] = term[rows, :].astype(BF16)
                hop(0, u, zpos + towards).start()
                continue
            if t < 3:
                hop(t - 1, u, zpos + backwards).wait_recv()
                chain_out[t, u] = (term[rows, :] + chain_in[t - 1, u].astype(F32)).astype(BF16)
            if t == 1:
                hop(1, u, zpos + backwards).start()
            if t == 2:
                @pl.when(even)
                def _():
                    hop(2, u, zpos + 7).start()

                @pl.when(jnp.logical_not(even))
                def _():
                    last_hop(2, u, 1).start()
            if t == 3:
                @pl.when(jnp.logical_not(even))
                def _():
                    hop(2, u, zpos + 1).wait_recv()
                    chain_out[3, u] = (term[rows, :] + chain_in[2, u].astype(F32)).astype(BF16)
                    last_hop(3, u, 0).start()

    own_half = pl.ds(pl.multiple_of(core * HALF, HALF), HALF)

    @pl.when(even)
    def _():
        mate_hop().start()
        proj_out[0] = term[own_half, :]

    contrib_down.wait()
    contrib_up.wait()
    right_out[0, 0] = contrib[...] + contrib_in[...]

    @pl.when(jnp.logical_not(even))
    def _():
        mate_hop().wait_recv()
        proj_out[0] = mate_in[...]

    for side in (1, 0):
        for v in range(PIECES // 2):
            rows = slice(v * PIECE, (v + 1) * PIECE)
            last_hop(2, v, side).wait_recv()
            proj_out[0, rows, :] += final_in[side, v].astype(F32)

    def drain_kv(j, _):
        spread_by = (j >= 6) & (j <= 7)

        @pl.when((j > 0) & jnp.where(spread_by, zpos + j <= 7, chip + j <= 15))
        def _():
            kv_copy(j).wait_send()

        @pl.when(j <= last)
        def _():
            forward(j).wait_send()
            part_copy(j).wait_send()

        @pl.when((j > 0) & (j <= last))
        def _():
            grad_copy(j).wait_send()

        return 0

    lax.fori_loop(0, SPAN + 1, drain_kv, 0)
    for j in (6, 7):
        @pl.when((half == 1) & (zpos + j >= SPAN))
        def _():
            spread(j).wait_send()

    kg_over.wait_send()
    kg_mate.wait_send()
    kg_pass.wait_send()
    for u in range(PIECES):
        for t in range(3):
            hop(t, u, zpos + 1).wait_send()

        @pl.when(jnp.logical_not(even))
        def _():
            last_hop(3, u, 0).wait_send()

    @pl.when(even)
    def _():
        mate_hop().wait_send()


def emit(dq, kv, proj, left, right, dq_out, kv_out, proj_out, left_out, right_out, sem, head_sem):
    copies = [
        pltpu.make_async_copy(src, dst, sem.at[k])
        for k, (src, dst) in enumerate(
            ((kv, kv_out), (proj, proj_out), (left, left_out), (right, right_out))
        )
    ]
    for h in range(HEADS):
        lanes = slice(h * HD, (h + 1) * HD)
        copies.append(
            pltpu.make_async_copy(dq.at[lanes, :], dq_out.at[0, :, lanes], head_sem.at[h])
        )
    for copy in copies:
        copy.start()
    for copy in copies:
        copy.wait()


def on_device(*args):
    any_spec = pl.BlockSpec(memory_space=pl.ANY)
    vmem = pl.BlockSpec(memory_space=pltpu.VMEM)
    dma = pltpu.SemaphoreType.DMA
    n = SPAN + 1
    rows = HEADS * TOK
    results = pl.pallas_call(
        kernel,
        out_shape=(
            pltpu.VMEM((rows, HD), F32),
            pltpu.VMEM((1, TOK, 2 * HD), F32),
            pltpu.VMEM((1, HALF, 2 * HD), F32),
            pltpu.VMEM((1, 2, 4, ROWS), F32),
            pltpu.VMEM((1, 1, 2, 4, 6144), F32),
        ),
        in_specs=[any_spec] * 9,
        out_specs=(vmem,) * 5,
        scratch_shapes=[
            pltpu.VMEM((TOK, HEADS * HD), BF16),
            pltpu.VMEM((TOK, HEADS * HD), BF16),
            pltpu.VMEM((TOK, HEADS * HD), BF16),
            pltpu.VMEM((HEADS, TOK), F32),
            pltpu.VMEM((ROWS, 6144), BF16),
            pltpu.VMEM((4, 6144), BF16),
            pltpu.VMEM((rows, HD), BF16),
            pltpu.VMEM((rows, HD), BF16),
            pltpu.VMEM((HD, rows), BF16),
            pltpu.VMEM((HD, rows), BF16),
            pltpu.VMEM((rows, HD), F32),
            pltpu.VMEM((rows, HD), F32),
            pltpu.VMEM((TOK, 2 * TOK), F32),
            pltpu.VMEM((n, 2 * TOK, 2 * HD), BF16),
            pltpu.VMEM((n, 2, 2 * HD, TOK), F32),
            pltpu.VMEM((n, 2 * HD, TOK), F32),
            pltpu.VMEM((n, 2 * HD, TOK), BF16),
            pltpu.VMEM((n, 2 * HD, TOK), BF16),
            pltpu.VMEM((2 * HD, TOK), F32),
            pltpu.VMEM((4 * TOK, 4 * ROWS), BF16),
            pltpu.VMEM((4, 2 * HD, TOK), BF16),
            pltpu.VMEM((ROWS, 2 * HD), F32),
            pltpu.VMEM((4, PIECES, PIECE, 2 * HD), BF16),
            pltpu.VMEM((3, PIECES, PIECE, 2 * HD), BF16),
            pltpu.VMEM((2, PIECES // 2, PIECE, 2 * HD), BF16),
            pltpu.VMEM((HALF, 2 * HD), F32),
            pltpu.VMEM((4, ROWS), F32),
            pltpu.VMEM((2, 4, ROWS), F32),
            pltpu.VMEM((2, 4, 6144), F32),
            pltpu.VMEM((2, 4, 6144), F32),
            dma((8,)),
            dma((n,)), dma((n,)), dma((3,)), dma((n,)), dma((n,)), dma((n,)), dma((n,)), dma((n,)), dma((n,)),
            dma((16,)), dma((16,)), dma((3,)), dma((4,)),
            dma((4, PIECES)), dma((3, PIECES)), dma((2, PIECES // 2)), dma, dma,
            dma((2,)), dma((2,)), dma((2,)), dma((2,)),
        ],
        compiler_params=pltpu.CompilerParams(
            collective_id=0, has_side_effects=True, vmem_limit_bytes=56 * 1024 * 1024
        ),
        name="fused",
    )(*args)
    return pl.pallas_call(
        emit,
        out_shape=(
            jax.ShapeDtypeStruct((1, TOK, HEADS * HD), F32),
            jax.ShapeDtypeStruct((1, TOK, 2 * HD), F32),
            jax.ShapeDtypeStruct((1, HALF, 2 * HD), F32),
            jax.ShapeDtypeStruct((1, 2, 4, ROWS), F32),
            jax.ShapeDtypeStruct((1, 1, 2, 4, 6144), F32),
        ),
        in_specs=[vmem] * 5,
        out_specs=(any_spec,) * 5,
        scratch_shapes=[dma((4,)), dma((HEADS,))],
        compiler_params=pltpu.CompilerParams(vmem_limit_bytes=4 * 1024 * 1024),
        name="emit",
    )(*results)


def solution(mesh):
    return jax.shard_map(
        on_device,
        mesh=mesh,
        in_specs=(
            P("rep", "seq", None),
            P("rep", "seq", None),
            P("rep", "seq", None),
            P("rep", "seq", None),
            P("rep", "seq", None),
            P("rep", None, "seq"),
            P("rep", "seq", None),
            P("rep", "seq", None),
            P("seq", None, None),
        ),
        out_specs=(
            P("rep", "seq", None),
            P("rep", "seq", None),
            P("rep", "seq", None),
            P("rep", None, None, "seq"),
            P("rep", "seq", None, None, None),
        ),
        check_vma=False,
    )
```
